32 devices in a mesh: rep: 8 (over z, x), shard: 4 (over y, core).
Axes of the slice: x: 2, y: 2, z: 4, core: 2. Of those that a mesh axis runs over, the one named last changes fastest.
Arguments:
- grads: bfloat16 [8, 12, 512, 512], P('rep', 'shard')
- owner_slot: int32 [12], replicated, may hold values from 0 to 11, as said below
- refresh: int32 [1], replicated, may hold values from 0 to 11
- left_stat: float32 [12, 512, 512], P('shard', 'rep'), as said below
- right_stat: float32 [12, 512, 512], P('shard', 'rep'), as said below
- left_root: bfloat16 [12, 512, 512], P('shard', 'rep'), as said below
- right_root: bfloat16 [12, 512, 512], P('shard'), as said below
Outputs:
- left_new: float32 [12, 512, 512], P('shard', 'rep')
- right_new: float32 [12, 512, 512], P('shard', 'rep')
- left_root_new: bfloat16 [12, 512, 512], P('shard', 'rep')
- right_root_new: bfloat16 [12, 512, 512], P('shard')
- direction: bfloat16 [12, 512, 512], P('shard')
The draws below stay inside these ranges and needn't reach their ends.
Inputs may be any that keep to these rules, and one draw needn't show every extreme that they name: A permutation: block b sits at position owner_slot[b] of owner order, which belongs to shard index owner_slot[b] // 3, with owner_slot[b] % 3 == b % 3; the 3 blocks s * 3 to s * 3 + 2 all go to different shard indices. `left_stat`: each block is symmetric positive definite. `right_stat`: each block is symmetric positive definite. `left_root`: each block is symmetric. `right_root`: each block is symmetric.
All inputs are finite; a program needn't handle non-finite values.
Results may differ from the reference program's by a relative error of at most 0.0004.
The reference program's roundings to bfloat16 on the way count: a program that leaves them out, or rounds other values in their place, can miss the bound.
Values may be sent and summed in bfloat16 or wider, within the bound.
A program may use at most 64 MiB of HBM per device.

```python
import jax
import jax.numpy as jnp
from jax import lax

BS = 512
BPS = 3
ITERS = 2
REFRESH = 1
NBLK = 12
N_REP = 8
N_SHARD = 4


def draw_grads(key, part):
    key_each = jax.random.fold_in(jax.random.fold_in(key, 3), 2)
    replica_keys = jax.random.split(key_each, N_REP)

    def one_replica(replica_key):
        return (jax.random.normal(replica_key, (NBLK, BS, BS)) * (1.0 / N_REP ** 0.5)).astype(jnp.bfloat16)
    return lax.map(one_replica, replica_keys)


def draw_owner_slot(key, part):
    key_outer, key_inner, key_shift = jax.random.split(jax.random.fold_in(key, 5), 3)
    outer_perm = jax.random.permutation(key_outer, N_SHARD)
    inner_perm = jax.random.permutation(key_inner, N_SHARD)
    shift_perm = jax.random.permutation(key_shift, N_SHARD)[:BPS]
    owners = outer_perm[(inner_perm[:, None] + shift_perm[None, :]) % N_SHARD]
    slot_ids = owners * BPS + jnp.arange(BPS, dtype=jnp.int32)[None, :]
    return slot_ids.reshape(-1).astype(jnp.int32)


def stat_blocks(key):
    key_base, key_scale = jax.random.split(key)
    factor_keys = jax.random.split(key_base, NBLK)
    identity = jnp.eye(BS, dtype=jnp.float32)

    def one_block(block_key):
        normal_part = jax.random.normal(block_key, (BS, BS))
        return jnp.dot(normal_part, normal_part.T) / BS + 0.5 * identity
    blocks = lax.map(one_block, factor_keys)
    row_scale = jnp.exp(jax.random.uniform(key_scale, (NBLK, BS, 1), minval=0.0, maxval=1.15))
    return blocks * row_scale * jnp.swapaxes(row_scale, 1, 2)


def root_blocks(key):
    key_diag, key_off = jax.random.split(key)
    diagonal_part = jnp.exp(jax.random.uniform(key_diag, (NBLK, BS), minval=-0.69, maxval=0.69))
    off_part = jax.random.normal(key_off, (NBLK, BS, BS)) * (0.7 / BS ** 0.5)
    symmetric = (off_part + jnp.swapaxes(off_part, 1, 2)) * 0.5
    return (symmetric + diagonal_part[:, :, None] * jnp.eye(BS, dtype=jnp.float32)).astype(jnp.bfloat16)


def draw_left_stat(key, part):
    return stat_blocks(jax.random.fold_in(key, 11))


def draw_right_stat(key, part):
    return stat_blocks(jax.random.fold_in(key, 13))


def draw_left_root(key, part):
    return root_blocks(jax.random.fold_in(key, 17))


def draw_right_root(key, part):
    return root_blocks(jax.random.fold_in(key, 19))


def setup_inputs(seed: int = 0) -> dict:
    key_of = jax.random.split(jax.random.key(seed), 8)
    grads = draw_grads(jax.random.fold_in(key_of[7], 71), 0)
    owner_slot = draw_owner_slot(jax.random.fold_in(key_of[7], 71), 0)
    refresh = jax.random.randint(key_of[2], (REFRESH,), 0, NBLK).astype(jnp.int32)
    left_stat = draw_left_stat(jax.random.fold_in(key_of[7], 71), 0)
    right_stat = draw_right_stat(jax.random.fold_in(key_of[7], 71), 0)
    left_root = draw_left_root(jax.random.fold_in(key_of[7], 71), 0)
    right_root = draw_right_root(jax.random.fold_in(key_of[7], 71), 0)
    return dict(grads=grads, owner_slot=owner_slot, refresh=refresh, left_stat=left_stat, right_stat=right_stat, left_root=left_root, right_root=right_root)


decay_rate = 0.95
epsilon_shift = 1e-06

def inverse_root(statistic):
    order = statistic.shape[0]
    identity = jnp.eye(order, dtype=jnp.float32)
    shifted = statistic + epsilon_shift * identity
    norm_scale = 2.5 / jnp.sqrt(jnp.sum(shifted * shifted))
    moment = norm_scale * shifted
    current = identity
    for number in range(ITERS):
        factor = (5.0 * identity - moment) * 0.25
        factor_low = factor.astype(jnp.bfloat16)
        if number == 0:
            current = jnp.sqrt(jnp.sqrt(norm_scale)) * factor
        else:
            current = jnp.dot(current.astype(jnp.bfloat16), factor_low, preferred_element_type=jnp.float32)
        if number + 1 < ITERS:
            square = jnp.dot(factor_low, factor_low, preferred_element_type=jnp.float32).astype(jnp.bfloat16)
            fourth = jnp.dot(square, square, preferred_element_type=jnp.float32).astype(jnp.bfloat16)
            moment = jnp.dot(fourth, moment.astype(jnp.bfloat16), preferred_element_type=jnp.float32)
    return current.astype(jnp.bfloat16)

def add_replica(running, piece):
    return (running + piece.astype(jnp.float32), None)

def reference(grads, owner_slot, refresh, left_stat, right_stat, left_root, right_root):
    summed, unused = lax.scan(add_replica, jnp.zeros((NBLK, BS, BS), jnp.float32), grads)
    gradient = summed.astype(jnp.bfloat16)
    owned_grad = jnp.zeros_like(gradient).at[owner_slot].set(gradient)
    owned_wide = owned_grad.astype(jnp.float32)
    highest = lax.Precision.HIGHEST
    left_new = decay_rate * left_stat + jnp.einsum('bij,bkj->bik', owned_wide, owned_wide, precision=highest) / BS
    right_new = decay_rate * right_stat + jnp.einsum('bji,bjk->bik', owned_wide, owned_wide, precision=highest) / BS
    fresh_slot = owner_slot[refresh[0]]
    fresh_left = inverse_root(left_new[fresh_slot])
    fresh_right = inverse_root(right_new[fresh_slot])
    left_root_new = left_root.at[fresh_slot].set(fresh_left)
    right_root_new = right_root.at[fresh_slot].set(fresh_right)
    half_step = jnp.einsum('bij,bjk->bik', left_root_new.astype(jnp.float32), owned_wide, precision=highest).astype(jnp.bfloat16)
    direction = jnp.einsum('bij,bjk->bik', half_step.astype(jnp.float32), right_root_new.astype(jnp.float32), precision=highest).astype(jnp.bfloat16)
    return (left_new, right_new, left_root_new, right_root_new, direction)
```

```python
import functools

import jax
import jax.numpy as jnp
from jax import lax
from jax.experimental import pallas as pl
from jax.experimental.pallas import tpu as pltpu
from jax.sharding import PartitionSpec as P

ITERS = 2


decay_rate = 0.95
epsilon_shift = 1e-06


def inverse_root(statistic):
    order = statistic.shape[0]
    identity = jnp.eye(order, dtype=jnp.float32)
    shifted = statistic + epsilon_shift * identity
    norm_scale = 2.5 / jnp.sqrt(jnp.sum(shifted * shifted))
    moment = norm_scale * shifted
    current = identity
    for number in range(ITERS):
        factor = (5.0 * identity - moment) * 0.25
        factor_low = factor.astype(jnp.bfloat16)
        if number == 0:
            current = jnp.sqrt(jnp.sqrt(norm_scale)) * factor
        else:
            current = jnp.dot(
                current.astype(jnp.bfloat16), factor_low, preferred_element_type=jnp.float32
            )
        if number + 1 < ITERS:
            square = jnp.dot(factor_low, factor_low, preferred_element_type=jnp.float32).astype(
                jnp.bfloat16
            )
            fourth = jnp.dot(square, square, preferred_element_type=jnp.float32).astype(
                jnp.bfloat16
            )
            moment = jnp.dot(
                fourth, moment.astype(jnp.bfloat16), preferred_element_type=jnp.float32
            )
    return current.astype(jnp.bfloat16)


def both_roots(fresh_whole):
    return (inverse_root(fresh_whole[0]), inverse_root(fresh_whole[1]))


def empty_roots(fresh_whole):
    blank = jnp.zeros(fresh_whole.shape[1:], jnp.bfloat16)
    return (blank, blank)


def body(grads, owner_slot, refresh, left_stat, right_stat, left_root, right_root):
    blocks = grads.shape[1]
    block_order = grads.shape[2]
    rep_count = lax.axis_size("rep")
    shards = lax.axis_size("shard")
    row_count = block_order // rep_count
    rep_index = lax.axis_index("rep")
    shard_index = lax.axis_index("shard")
    partial_value = grads[0].astype(jnp.float32)
    row_share = lax.psum_scatter(partial_value, "rep", scatter_dimension=1, tiled=True)
    row_share = row_share.astype(jnp.bfloat16)
    slot_table = owner_slot.reshape(shards, blocks)
    own_slots = lax.dynamic_index_in_dim(slot_table, shard_index, 0, keepdims=False)
    targets = own_slots // blocks
    selector = (targets[None, :] == jnp.arange(shards, dtype=jnp.int32)[:, None]).astype(
        jnp.bfloat16
    )
    outgoing = jnp.einsum(
        "ok,krc->orc", selector, row_share, preferred_element_type=jnp.float32
    ).astype(jnp.bfloat16)
    incoming = lax.all_to_all(outgoing, "shard", split_axis=0, concat_axis=0, tiled=True)
    wanted = shard_index * blocks + jnp.arange(blocks, dtype=jnp.int32)
    receiver = (jnp.transpose(slot_table) == wanted[:, None]).astype(jnp.bfloat16)
    owned_rows = jnp.einsum(
        "ks,src->krc", receiver, incoming, preferred_element_type=jnp.float32
    ).astype(jnp.bfloat16)
    gathered = lax.all_gather(owned_rows, "rep", axis=1, tiled=True)
    left_new = (
        decay_rate * left_stat
        + jnp.einsum("krc,kjc->krj", owned_rows, gathered, preferred_element_type=jnp.float32)
        / block_order
    )
    column_share = lax.dynamic_slice_in_dim(gathered, rep_index * row_count, row_count, 2)
    right_new = (
        decay_rate * right_stat
        + jnp.einsum("kic,kij->kcj", column_share, gathered, preferred_element_type=jnp.float32)
        / block_order
    )
    fresh_slot = owner_slot[refresh[0]]
    holder = fresh_slot // blocks
    slot_index = fresh_slot % blocks
    owns_fresh = holder == shard_index
    fresh_pair = jnp.stack(
        [
            lax.dynamic_index_in_dim(left_new, slot_index, 0, keepdims=False),
            lax.dynamic_index_in_dim(right_new, slot_index, 0, keepdims=False),
        ]
    )
    fresh_whole = lax.all_gather(fresh_pair, "rep", axis=1, tiled=True)
    fresh_left, fresh_right = lax.cond(owns_fresh, both_roots, empty_roots, fresh_whole)
    fresh_rows = lax.dynamic_slice_in_dim(fresh_left, rep_index * row_count, row_count, 0)
    left_updated = lax.dynamic_update_index_in_dim(left_root, fresh_rows, slot_index, 0)
    left_root_new = jnp.where(owns_fresh, left_updated, left_root)
    right_updated = lax.dynamic_update_index_in_dim(right_root, fresh_right, slot_index, 0)
    right_root_new = jnp.where(owns_fresh, right_updated, right_root)
    half_step = jnp.einsum(
        "kri,kic->krc", left_root_new, gathered, preferred_element_type=jnp.float32
    ).astype(jnp.bfloat16)
    preconditioned = jnp.einsum(
        "kri,kic->krc", half_step, right_root_new, preferred_element_type=jnp.float32
    ).astype(jnp.bfloat16)
    direction = lax.all_gather(preconditioned, "rep", axis=1, tiled=True)
    return (left_new, right_new, left_root_new, right_root_new, direction)


MESH = pl.DeviceIdType.MESH


def exchange_kernel(
    reps,
    shards,
    slots_ref,
    grads_ref,
    left_ref,
    stat_ref,
    owned_ref,
    grad_full,
    left_full,
    stat_full,
    pieces,
    share,
    outgoing,
    incoming,
    sum_send,
    sum_recv,
    swap_send,
    swap_recv,
    line_send,
    line_recv,
    local_sem,
):
    blocks = grads_ref.shape[1]
    rows = grads_ref.shape[2] // reps
    length = reps // 2
    me = lax.axis_index("rep")
    shard = lax.axis_index("shard")
    place = me // 2
    side = me % 2
    partner = place * 2 + (1 - side)

    def span(index):
        return pl.ds(pl.multiple_of(index * rows, rows), rows)

    barrier = pltpu.get_barrier_semaphore()
    for step in range(1, reps):
        pl.semaphore_signal(
            barrier, inc=1, device_id=((me + step) % reps, shard), device_id_type=MESH
        )
    for step in range(1, shards):
        pl.semaphore_signal(
            barrier, inc=1, device_id=(me, (shard + step) % shards), device_id_type=MESH
        )
    pl.semaphore_wait(barrier, reps + shards - 2)

    sums = []
    for step in SUM_ORDER(reps):
        peer = (me + step) % reps
        copy = pltpu.make_async_remote_copy(
            src_ref=grads_ref.at[0, :, span(peer), :],
            dst_ref=pieces.at[me],
            send_sem=sum_send.at[step],
            recv_sem=sum_recv.at[step],
            device_id=(peer, shard),
            device_id_type=MESH,
        )
        copy.start()
        sums.append(copy)

    fulls = (left_full, stat_full, grad_full)

    def line_copy(array, source, way, target, first):
        full = fulls[array]
        origin = first if first is not None else full.at[:, span(source), :]
        return pltpu.make_async_remote_copy(
            src_ref=origin,
            dst_ref=full.at[:, span(source), :],
            send_sem=line_send.at[array, source, way],
            recv_sem=line_recv.at[array, source],
            device_id=(target, shard),
            device_id_type=MESH,
        )

    ways = ((0, 1), (1, -1))

    def send_line(array, source, way, delta, first):
        inside = (place + delta >= 0) & (place + delta < length)

        @pl.when(inside)
        def _():
            line_copy(array, source, way, me + 2 * delta, first).start()

    def wait_line(array, source, way, delta, first):
        inside = (place + delta >= 0) & (place + delta < length)

        @pl.when(inside)
        def _():
            line_copy(array, source, way, me + 2 * delta, first).wait_send()

    def begin(array, first):
        for way, delta in ways:
            send_line(array, me, way, delta, first)
        line_copy(array, me, 2, partner, first).start()

    def forward(array, hop):
        for way, delta in ways:
            origin = place - delta * hop

            @pl.when((origin >= 0) & (origin < length))
            def _():
                source = origin * 2 + side
                line_copy(array, source, 2, partner, None).wait_recv()
                send_line(array, source, way, delta, None)
                line_copy(array, source, 2, partner, None).start()

    def finish(array, first):
        for other in range(length):
            line_copy(array, other * 2 + 1 - side, 2, partner, None).wait_recv()
        for way, delta in ways:
            wait_line(array, me, way, delta, first)
        line_copy(array, me, 2, partner, first).wait_send()
        for hop in range(1, length):
            for way, delta in ways:
                origin = place - delta * hop

                @pl.when((origin >= 0) & (origin < length))
                def _():
                    source = origin * 2 + side
                    wait_line(array, source, way, delta, None)
                    line_copy(array, source, 2, partner, None).wait_send()

    begin(0, left_ref)
    begin(1, stat_ref)
    own_left = pltpu.make_async_copy(left_ref, left_full.at[:, span(me), :], local_sem.at[0])
    own_left.start()
    own_stat = pltpu.make_async_copy(stat_ref, stat_full.at[:, span(me), :], local_sem.at[1])
    own_stat.start()

    pieces[me] = grads_ref[0, :, span(me), :]
    for copy in sums:
        copy.wait_recv()
    for block in range(blocks):
        total = pieces[0, block].astype(jnp.float32)
        for index in range(1, reps):
            total = total + pieces[index, block].astype(jnp.float32)
        share[block] = total.astype(jnp.bfloat16)

    for target in range(shards):
        chosen = jnp.int32(0)
        for block in range(1, blocks):
            chosen = jnp.where(
                slots_ref[shard * blocks + block] // blocks == target, jnp.int32(block), chosen
            )
        outgoing[target] = share[chosen]
    swaps = []
    for step in range(1, shards):
        peer = (shard + step) % shards
        copy = pltpu.make_async_remote_copy(
            src_ref=outgoing.at[peer],
            dst_ref=incoming.at[shard],
            send_sem=swap_send.at[step],
            recv_sem=swap_recv.at[step],
            device_id=(me, peer),
            device_id_type=MESH,
        )
        copy.start()
        swaps.append(copy)
    incoming[shard] = outgoing[shard]
    for copy in swaps:
        copy.wait_recv()
    for block in range(blocks):
        holder = jnp.int32(0)
        for origin in range(1, shards):
            holder = jnp.where(
                slots_ref[origin * blocks + block] == shard * blocks + block,
                jnp.int32(origin),
                holder,
            )
        value = incoming[holder]
        owned_ref[block] = value
        grad_full[block, span(me), :] = value
    begin(2, owned_ref)
    for hop in range(1, length):
        for array in range(3):
            forward(array, hop)
    for array, first in enumerate((left_ref, stat_ref, owned_ref)):
        finish(array, first)
    own_left.wait()
    own_stat.wait()
    for copy in sums + swaps:
        copy.wait_send()


def SUM_ORDER(reps):
    return range(1, reps)


def exchange(owner_slot, grads, left_root, fresh_stats, reps, shards):
    blocks, order = grads.shape[1], grads.shape[2]
    rows = order // reps
    low = jnp.bfloat16
    vmem = pl.BlockSpec(memory_space=pltpu.VMEM)
    return pl.pallas_call(
        functools.partial(exchange_kernel, reps, shards),
        out_shape=(
            jax.ShapeDtypeStruct((blocks, rows, order), low),
            jax.ShapeDtypeStruct((blocks, order, order), low),
            jax.ShapeDtypeStruct((blocks, order, order), low),
            jax.ShapeDtypeStruct((2, order, order), low),
        ),
        in_specs=[pl.BlockSpec(memory_space=pltpu.SMEM), vmem, vmem, vmem],
        out_specs=(vmem, vmem, vmem, vmem),
        scratch_shapes=[
            pltpu.VMEM((reps, blocks, rows, order), low),
            pltpu.VMEM((blocks, rows, order), low),
            pltpu.VMEM((shards, rows, order), low),
            pltpu.VMEM((shards, rows, order), low),
            pltpu.SemaphoreType.DMA((reps,)),
            pltpu.SemaphoreType.DMA((reps,)),
            pltpu.SemaphoreType.DMA((shards,)),
            pltpu.SemaphoreType.DMA((shards,)),
            pltpu.SemaphoreType.DMA((3, reps, 3)),
            pltpu.SemaphoreType.DMA((3, reps)),
            pltpu.SemaphoreType.DMA((2,)),
        ],
        compiler_params=pltpu.CompilerParams(collective_id=0, has_side_effects=True),
    )(owner_slot, grads, left_root, fresh_stats)


def direct_body(grads, owner_slot, refresh, left_stat, right_stat, left_root, right_root):
    blocks = grads.shape[1]
    block_order = grads.shape[2]
    rep_count = lax.axis_size("rep")
    shards = lax.axis_size("shard")
    row_count = block_order // rep_count
    rep_index = lax.axis_index("rep")
    shard_index = lax.axis_index("shard")
    fresh_slot = owner_slot[refresh[0]]
    slot_index = fresh_slot % blocks
    owns_fresh = fresh_slot // blocks == shard_index
    fresh_stats = jnp.stack(
        [
            lax.dynamic_index_in_dim(left_stat, slot_index, 0, keepdims=False),
            lax.dynamic_index_in_dim(right_stat, slot_index, 0, keepdims=False),
        ]
    ).astype(jnp.bfloat16)
    owned_rows, gathered, left_full, stat_full = exchange(
        owner_slot, grads, left_root, fresh_stats, rep_count, shards
    )
    left_new = (
        decay_rate * left_stat
        + jnp.einsum("krc,kjc->krj", owned_rows, gathered, preferred_element_type=jnp.float32)
        / block_order
    )
    column_share = lax.dynamic_slice_in_dim(gathered, rep_index * row_count, row_count, 2)
    right_new = (
        decay_rate * right_stat
        + jnp.einsum("kic,kij->kcj", column_share, gathered, preferred_element_type=jnp.float32)
        / block_order
    )
    grad_fresh = lax.dynamic_index_in_dim(gathered, slot_index, 0, keepdims=False)

    def renew(operands):
        grad, stats = operands
        wide = stats.astype(jnp.float32)
        left = (
            decay_rate * wide[0]
            + jnp.einsum("ic,jc->ij", grad, grad, preferred_element_type=jnp.float32) / block_order
        )
        right = (
            decay_rate * wide[1]
            + jnp.einsum("ci,cj->ij", grad, grad, preferred_element_type=jnp.float32) / block_order
        )
        return inverse_root(left), inverse_root(right)

    def skip(operands):
        blank = jnp.zeros((block_order, block_order), jnp.bfloat16)
        return blank, blank

    fresh_left, fresh_right = lax.cond(owns_fresh, renew, skip, (grad_fresh, stat_full))
    left_all = jnp.where(
        owns_fresh, lax.dynamic_update_index_in_dim(left_full, fresh_left, slot_index, 0), left_full
    )
    fresh_rows = lax.dynamic_slice_in_dim(fresh_left, rep_index * row_count, row_count, 0)
    left_updated = lax.dynamic_update_index_in_dim(left_root, fresh_rows, slot_index, 0)
    left_root_new = jnp.where(owns_fresh, left_updated, left_root)
    right_updated = lax.dynamic_update_index_in_dim(right_root, fresh_right, slot_index, 0)
    right_root_new = jnp.where(owns_fresh, right_updated, right_root)
    half_step = jnp.einsum(
        "kri,kic->krc", left_all, gathered, preferred_element_type=jnp.float32
    ).astype(jnp.bfloat16)
    direction = jnp.einsum(
        "kri,kic->krc", half_step, right_root_new, preferred_element_type=jnp.float32
    ).astype(jnp.bfloat16)
    return (left_new, right_new, left_root_new, right_root_new, direction)


def choose(mesh, *arrays):
    reps = mesh.shape["rep"]
    rows = arrays[0].shape[2] // reps
    direct = reps % 2 == 0 and rows % 16 == 0
    return (direct_body if direct else body)


def solution(mesh):
    def run(*arrays):
        return mapped(mesh, choose(mesh, *arrays))(*arrays)

    return run


def mapped(mesh, body):
    return jax.shard_map(
        body,
        mesh=mesh,
        in_specs=(
            P("rep", "shard", None, None),
            P(),
            P(),
            P("shard", "rep", None),
            P("shard", "rep", None),
            P("shard", "rep", None),
            P("shard", None, None),
        ),
        out_specs=(
            P("shard", "rep", None),
            P("shard", "rep", None),
            P("shard", "rep", None),
            P("shard", None, None),
            P("shard", None, None),
        ),
        check_vma=False,
    )
```

```python
import functools

import jax
import jax.numpy as jnp
from jax import lax
from jax.experimental import pallas as pl
from jax.experimental.pallas import tpu as pltpu
from jax.sharding import PartitionSpec as P

ITERS = 2


decay_rate = 0.95
epsilon_shift = 1e-06


def inverse_root(statistic):
    order = statistic.shape[0]
    identity = (
        lax.broadcasted_iota(jnp.int32, (order, order), 0)
        == lax.broadcasted_iota(jnp.int32, (order, order), 1)
    ).astype(jnp.float32)
    shifted = statistic + epsilon_shift * identity
    norm_scale = 2.5 / jnp.sqrt(jnp.sum(shifted * shifted))
    moment = norm_scale * shifted
    current = identity
    for number in range(ITERS):
        factor = (5.0 * identity - moment) * 0.25
        factor_low = factor.astype(jnp.bfloat16)
        if number == 0:
            current = jnp.sqrt(jnp.sqrt(norm_scale)) * factor
        else:
            current = jnp.dot(
                current.astype(jnp.bfloat16), factor_low, preferred_element_type=jnp.float32
            )
        if number + 1 < ITERS:
            square = jnp.dot(factor_low, factor_low, preferred_element_type=jnp.float32).astype(
                jnp.bfloat16
            )
            fourth = jnp.dot(square, square, preferred_element_type=jnp.float32).astype(
                jnp.bfloat16
            )
            moment = jnp.dot(
                fourth, moment.astype(jnp.bfloat16), preferred_element_type=jnp.float32
            )
    return current.astype(jnp.bfloat16)


def both_roots(fresh_whole):
    return (inverse_root(fresh_whole[0]), inverse_root(fresh_whole[1]))


def empty_roots(fresh_whole):
    blank = jnp.zeros(fresh_whole.shape[1:], jnp.bfloat16)
    return (blank, blank)


def body(grads, owner_slot, refresh, left_stat, right_stat, left_root, right_root):
    blocks = grads.shape[1]
    block_order = grads.shape[2]
    rep_count = lax.axis_size("rep")
    shards = lax.axis_size("shard")
    row_count = block_order // rep_count
    rep_index = lax.axis_index("rep")
    shard_index = lax.axis_index("shard")
    partial_value = grads[0].astype(jnp.float32)
    row_share = lax.psum_scatter(partial_value, "rep", scatter_dimension=1, tiled=True)
    row_share = row_share.astype(jnp.bfloat16)
    slot_table = owner_slot.reshape(shards, blocks)
    own_slots = lax.dynamic_index_in_dim(slot_table, shard_index, 0, keepdims=False)
    targets = own_slots // blocks
    selector = (targets[None, :] == jnp.arange(shards, dtype=jnp.int32)[:, None]).astype(
        jnp.bfloat16
    )
    outgoing = jnp.einsum(
        "ok,krc->orc", selector, row_share, preferred_element_type=jnp.float32
    ).astype(jnp.bfloat16)
    incoming = lax.all_to_all(outgoing, "shard", split_axis=0, concat_axis=0, tiled=True)
    wanted = shard_index * blocks + jnp.arange(blocks, dtype=jnp.int32)
    receiver = (jnp.transpose(slot_table) == wanted[:, None]).astype(jnp.bfloat16)
    owned_rows = jnp.einsum(
        "ks,src->krc", receiver, incoming, preferred_element_type=jnp.float32
    ).astype(jnp.bfloat16)
    gathered = lax.all_gather(owned_rows, "rep", axis=1, tiled=True)
    left_new = (
        decay_rate * left_stat
        + jnp.einsum("krc,kjc->krj", owned_rows, gathered, preferred_element_type=jnp.float32)
        / block_order
    )
    column_share = lax.dynamic_slice_in_dim(gathered, rep_index * row_count, row_count, 2)
    right_new = (
        decay_rate * right_stat
        + jnp.einsum("kic,kij->kcj", column_share, gathered, preferred_element_type=jnp.float32)
        / block_order
    )
    fresh_slot = owner_slot[refresh[0]]
    holder = fresh_slot // blocks
    slot_index = fresh_slot % blocks
    owns_fresh = holder == shard_index
    fresh_pair = jnp.stack(
        [
            lax.dynamic_index_in_dim(left_new, slot_index, 0, keepdims=False),
            lax.dynamic_index_in_dim(right_new, slot_index, 0, keepdims=False),
        ]
    )
    fresh_whole = lax.all_gather(fresh_pair, "rep", axis=1, tiled=True)
    fresh_left, fresh_right = lax.cond(owns_fresh, both_roots, empty_roots, fresh_whole)
    fresh_rows = lax.dynamic_slice_in_dim(fresh_left, rep_index * row_count, row_count, 0)
    left_updated = lax.dynamic_update_index_in_dim(left_root, fresh_rows, slot_index, 0)
    left_root_new = jnp.where(owns_fresh, left_updated, left_root)
    right_updated = lax.dynamic_update_index_in_dim(right_root, fresh_right, slot_index, 0)
    right_root_new = jnp.where(owns_fresh, right_updated, right_root)
    half_step = jnp.einsum(
        "kri,kic->krc", left_root_new, gathered, preferred_element_type=jnp.float32
    ).astype(jnp.bfloat16)
    preconditioned = jnp.einsum(
        "kri,kic->krc", half_step, right_root_new, preferred_element_type=jnp.float32
    ).astype(jnp.bfloat16)
    direction = lax.all_gather(preconditioned, "rep", axis=1, tiled=True)
    return (left_new, right_new, left_root_new, right_root_new, direction)


MESH = pl.DeviceIdType.MESH


def exchange_kernel(
    reps,
    shards,
    slots_ref,
    refresh_ref,
    grads_ref,
    left_ref,
    left_stat_ref,
    right_stat_ref,
    owned_ref,
    grad_full,
    left_full,
    stat_full,
    stat_ref,
    pieces,
    share,
    outgoing,
    incoming,
    sum_send,
    sum_recv,
    swap_send,
    swap_recv,
    line_send,
    line_recv,
    local_sem,
):
    blocks = grads_ref.shape[1]
    rows = grads_ref.shape[2] // reps
    length = reps // 2
    me = lax.axis_index("rep")
    shard = lax.axis_index("shard")
    place = me // 2
    side = me % 2
    partner = place * 2 + (1 - side)

    def span(index):
        return pl.ds(pl.multiple_of(index * rows, rows), rows)

    barrier = pltpu.get_barrier_semaphore()
    for step in range(1, reps):
        pl.semaphore_signal(
            barrier, inc=1, device_id=((me + step) % reps, shard), device_id_type=MESH
        )
    for step in range(1, shards):
        pl.semaphore_signal(
            barrier, inc=1, device_id=(me, (shard + step) % shards), device_id_type=MESH
        )
    pl.semaphore_wait(barrier, reps + shards - 2)

    sums = []
    for step in SUM_ORDER(reps):
        peer = (me + step) % reps
        copy = pltpu.make_async_remote_copy(
            src_ref=grads_ref.at[0, :, span(peer), :],
            dst_ref=pieces.at[me],
            send_sem=sum_send.at[step],
            recv_sem=sum_recv.at[step],
            device_id=(peer, shard),
            device_id_type=MESH,
        )
        copy.start()
        sums.append(copy)

    fulls = (left_full, stat_full, grad_full)

    def line_copy(array, source, way, target, first):
        full = fulls[array]
        origin = first if first is not None else full.at[:, span(source), :]
        return pltpu.make_async_remote_copy(
            src_ref=origin,
            dst_ref=full.at[:, span(source), :],
            send_sem=line_send.at[array, source, way],
            recv_sem=line_recv.at[array, source],
            device_id=(target, shard),
            device_id_type=MESH,
        )

    ways = ((0, 1), (1, -1))

    def send_line(array, source, way, delta, first):
        inside = (place + delta >= 0) & (place + delta < length)

        @pl.when(inside)
        def _():
            line_copy(array, source, way, me + 2 * delta, first).start()

    def wait_line(array, source, way, delta, first):
        inside = (place + delta >= 0) & (place + delta < length)

        @pl.when(inside)
        def _():
            line_copy(array, source, way, me + 2 * delta, first).wait_send()

    def begin(array, first):
        for way, delta in ways:
            send_line(array, me, way, delta, first)
        line_copy(array, me, 2, partner, first).start()

    def forward(array, hop):
        for way, delta in ways:
            origin = place - delta * hop

            @pl.when((origin >= 0) & (origin < length))
            def _():
                source = origin * 2 + side
                line_copy(array, source, 2, partner, None).wait_recv()
                send_line(array, source, way, delta, None)
                line_copy(array, source, 2, partner, None).start()

    def finish(array, first):
        for other in range(length):
            line_copy(array, other * 2 + 1 - side, 2, partner, None).wait_recv()
        for way, delta in ways:
            wait_line(array, me, way, delta, first)
        line_copy(array, me, 2, partner, first).wait_send()
        for hop in range(1, length):
            for way, delta in ways:
                origin = place - delta * hop

                @pl.when((origin >= 0) & (origin < length))
                def _():
                    source = origin * 2 + side
                    wait_line(array, source, way, delta, None)
                    line_copy(array, source, 2, partner, None).wait_send()

    slot = slots_ref[refresh_ref[0]] % blocks
    stat_ref[0] = left_stat_ref[slot].astype(jnp.bfloat16)
    stat_ref[1] = right_stat_ref[slot].astype(jnp.bfloat16)
    begin(0, left_ref)
    begin(1, stat_ref)
    own_left = pltpu.make_async_copy(left_ref, left_full.at[:, span(me), :], local_sem.at[0])
    own_left.start()
    own_stat = pltpu.make_async_copy(stat_ref, stat_full.at[:, span(me), :], local_sem.at[1])
    own_stat.start()

    pieces[me] = grads_ref[0, :, span(me), :]
    for copy in sums:
        copy.wait_recv()
    for block in range(blocks):
        total = pieces[0, block].astype(jnp.float32)
        for index in range(1, reps):
            total = total + pieces[index, block].astype(jnp.float32)
        share[block] = total.astype(jnp.bfloat16)

    for target in range(shards):
        chosen = jnp.int32(0)
        for block in range(1, blocks):
            chosen = jnp.where(
                slots_ref[shard * blocks + block] // blocks == target, jnp.int32(block), chosen
            )
        outgoing[target] = share[chosen]
    swaps = []
    for step in range(1, shards):
        peer = (shard + step) % shards
        copy = pltpu.make_async_remote_copy(
            src_ref=outgoing.at[peer],
            dst_ref=incoming.at[shard],
            send_sem=swap_send.at[step],
            recv_sem=swap_recv.at[step],
            device_id=(me, peer),
            device_id_type=MESH,
        )
        copy.start()
        swaps.append(copy)
    incoming[shard] = outgoing[shard]
    for copy in swaps:
        copy.wait_recv()
    for block in range(blocks):
        holder = jnp.int32(0)
        for origin in range(1, shards):
            holder = jnp.where(
                slots_ref[origin * blocks + block] == shard * blocks + block,
                jnp.int32(origin),
                holder,
            )
        value = incoming[holder]
        owned_ref[block] = value
        grad_full[block, span(me), :] = value
    begin(2, owned_ref)
    for hop in range(1, length):
        for array in range(3):
            forward(array, hop)
    for array, first in enumerate((left_ref, stat_ref, owned_ref)):
        finish(array, first)
    own_left.wait()
    own_stat.wait()
    for copy in sums + swaps:
        copy.wait_send()


def SUM_ORDER(reps):
    return range(1, reps)


def exchange(owner_slot, refresh, grads, left_root, left_stat, right_stat, reps, shards):
    blocks, order = grads.shape[1], grads.shape[2]
    rows = order // reps
    low = jnp.bfloat16
    vmem = pl.BlockSpec(memory_space=pltpu.VMEM)
    smem = pl.BlockSpec(memory_space=pltpu.SMEM)
    return pl.pallas_call(
        functools.partial(exchange_kernel, reps, shards),
        out_shape=(
            jax.ShapeDtypeStruct((blocks, rows, order), low),
            jax.ShapeDtypeStruct((blocks, order, order), low),
            jax.ShapeDtypeStruct((blocks, order, order), low),
            jax.ShapeDtypeStruct((2, order, order), low),
        ),
        in_specs=[smem, smem, vmem, vmem, vmem, vmem],
        out_specs=(vmem, vmem, vmem, vmem),
        scratch_shapes=[
            pltpu.VMEM((2, rows, order), low),
            pltpu.VMEM((reps, blocks, rows, order), low),
            pltpu.VMEM((blocks, rows, order), low),
            pltpu.VMEM((shards, rows, order), low),
            pltpu.VMEM((shards, rows, order), low),
            pltpu.SemaphoreType.DMA((reps,)),
            pltpu.SemaphoreType.DMA((reps,)),
            pltpu.SemaphoreType.DMA((shards,)),
            pltpu.SemaphoreType.DMA((shards,)),
            pltpu.SemaphoreType.DMA((3, reps, 3)),
            pltpu.SemaphoreType.DMA((3, reps)),
            pltpu.SemaphoreType.DMA((2,)),
        ],
        compiler_params=pltpu.CompilerParams(collective_id=0, has_side_effects=True),
    )(owner_slot, refresh, grads, left_root, left_stat, right_stat)


def dot(left, right, dims=(1, 0)):
    return lax.dot_general(
        left, right, (((dims[0],), (dims[1],)), ((), ())), preferred_element_type=jnp.float32
    )


def precondition_kernel(
    slots_ref,
    refresh_ref,
    owned_ref,
    grad_full,
    left_full,
    stat_full,
    left_stat_ref,
    right_stat_ref,
    left_ref,
    right_ref,
    left_new_ref,
    right_new_ref,
    left_root_ref,
    right_root_ref,
    direction_ref,
    turned,
    fresh_left,
):
    blocks, rows, order = owned_ref.shape
    me = lax.axis_index("rep")
    shard = lax.axis_index("shard")
    mine = pl.ds(pl.multiple_of(me * rows, rows), rows)
    fresh_slot = slots_ref[refresh_ref[0]]
    slot = fresh_slot % blocks
    owns = fresh_slot // blocks == shard
    for block in range(blocks):
        grad = grad_full[block]
        turned[block] = grad.T
        left_new_ref[block] = (
            decay_rate * left_stat_ref[block] + dot(owned_ref[block], grad, (1, 1)) / order
        )
        right_new_ref[block] = (
            decay_rate * right_stat_ref[block] + dot(turned[block, mine, :], grad) / order
        )
    left_root_ref[...] = left_ref[...]
    right_root_ref[...] = right_ref[...]

    @pl.when(owns)
    def _():
        grad = grad_full[slot]
        grad_turned = turned[slot]
        left = decay_rate * stat_full[0].astype(jnp.float32) + dot(grad, grad_turned) / order
        right = decay_rate * stat_full[1].astype(jnp.float32) + dot(grad_turned, grad) / order
        fresh_left[...] = inverse_root(left)
        left_root_ref[slot] = fresh_left[mine, :]
        right_root_ref[slot] = inverse_root(right)

    for block in range(blocks):
        replaced = owns & (slot == block)

        @pl.when(replaced)
        def _():
            half = dot(fresh_left[...], grad_full[block]).astype(jnp.bfloat16)
            direction_ref[block] = half

        @pl.when(jnp.logical_not(replaced))
        def _():
            half = dot(left_full[block], grad_full[block]).astype(jnp.bfloat16)
            direction_ref[block] = half

        direction_ref[block] = dot(direction_ref[block], right_root_ref[block]).astype(
            jnp.bfloat16
        )


def precondition(*operands):
    owned, grad_full = operands[2], operands[3]
    left_stat, left_root, right_root = operands[6], operands[8], operands[9]
    order = owned.shape[2]
    low = jnp.bfloat16
    vmem = pl.BlockSpec(memory_space=pltpu.VMEM)
    smem = pl.BlockSpec(memory_space=pltpu.SMEM)
    return pl.pallas_call(
        precondition_kernel,
        out_shape=(
            jax.ShapeDtypeStruct(left_stat.shape, jnp.float32),
            jax.ShapeDtypeStruct(left_stat.shape, jnp.float32),
            jax.ShapeDtypeStruct(left_root.shape, low),
            jax.ShapeDtypeStruct(right_root.shape, low),
            jax.ShapeDtypeStruct(right_root.shape, low),
        ),
        in_specs=[smem, smem] + [vmem] * 8,
        out_specs=(vmem,) * 5,
        scratch_shapes=[pltpu.VMEM(grad_full.shape, low), pltpu.VMEM((order, order), low)],
    )(*operands)


def direct_body(grads, owner_slot, refresh, left_stat, right_stat, left_root, right_root):
    gathered = exchange(
        owner_slot,
        refresh,
        grads,
        left_root,
        left_stat,
        right_stat,
        lax.axis_size("rep"),
        lax.axis_size("shard"),
    )
    return precondition(
        owner_slot, refresh, *gathered, left_stat, right_stat, left_root, right_root
    )


def choose(mesh, *arrays):
    reps = mesh.shape["rep"]
    rows = arrays[0].shape[2] // reps
    direct = reps % 2 == 0 and rows % 16 == 0
    return (direct_body if direct else body)


def solution(mesh):
    def run(*arrays):
        return mapped(mesh, choose(mesh, *arrays))(*arrays)

    return run


def mapped(mesh, body):
    return jax.shard_map(
        body,
        mesh=mesh,
        in_specs=(
            P("rep", "shard", None, None),
            P(),
            P(),
            P("shard", "rep", None),
            P("shard", "rep", None),
            P("shard", "rep", None),
            P("shard", None, None),
        ),
        out_specs=(
            P("shard", "rep", None),
            P("shard", "rep", None),
            P("shard", "rep", None),
            P("shard", None, None),
            P("shard", None, None),
        ),
        check_vma=False,
    )
```

```python
import functools

import jax
import jax.numpy as jnp
from jax import lax
from jax.experimental import pallas as pl
from jax.experimental.pallas import tpu as pltpu
from jax.sharding import PartitionSpec as P

ITERS = 2


decay_rate = 0.95
epsilon_shift = 1e-06


def inverse_root(statistic):
    order = statistic.shape[0]
    identity = (
        lax.broadcasted_iota(jnp.int32, (order, order), 0)
        == lax.broadcasted_iota(jnp.int32, (order, order), 1)
    ).astype(jnp.float32)
    shifted = statistic + epsilon_shift * identity
    norm_scale = 2.5 / jnp.sqrt(jnp.sum(shifted * shifted))
    moment = norm_scale * shifted
    current = identity
    for number in range(ITERS):
        factor = (5.0 * identity - moment) * 0.25
        factor_low = factor.astype(jnp.bfloat16)
        if number == 0:
            current = jnp.sqrt(jnp.sqrt(norm_scale)) * factor
        else:
            current = jnp.dot(
                current.astype(jnp.bfloat16), factor_low, preferred_element_type=jnp.float32
            )
        if number + 1 < ITERS:
            square = jnp.dot(factor_low, factor_low, preferred_element_type=jnp.float32).astype(
                jnp.bfloat16
            )
            fourth = jnp.dot(square, square, preferred_element_type=jnp.float32).astype(
                jnp.bfloat16
            )
            moment = jnp.dot(
                fourth, moment.astype(jnp.bfloat16), preferred_element_type=jnp.float32
            )
    return current.astype(jnp.bfloat16)


def both_roots(fresh_whole):
    return (inverse_root(fresh_whole[0]), inverse_root(fresh_whole[1]))


def empty_roots(fresh_whole):
    blank = jnp.zeros(fresh_whole.shape[1:], jnp.bfloat16)
    return (blank, blank)


def body(grads, owner_slot, refresh, left_stat, right_stat, left_root, right_root):
    blocks = grads.shape[1]
    block_order = grads.shape[2]
    rep_count = lax.axis_size("rep")
    shards = lax.axis_size("shard")
    row_count = block_order // rep_count
    rep_index = lax.axis_index("rep")
    shard_index = lax.axis_index("shard")
    partial_value = grads[0].astype(jnp.float32)
    row_share = lax.psum_scatter(partial_value, "rep", scatter_dimension=1, tiled=True)
    row_share = row_share.astype(jnp.bfloat16)
    slot_table = owner_slot.reshape(shards, blocks)
    own_slots = lax.dynamic_index_in_dim(slot_table, shard_index, 0, keepdims=False)
    targets = own_slots // blocks
    selector = (targets[None, :] == jnp.arange(shards, dtype=jnp.int32)[:, None]).astype(
        jnp.bfloat16
    )
    outgoing = jnp.einsum(
        "ok,krc->orc", selector, row_share, preferred_element_type=jnp.float32
    ).astype(jnp.bfloat16)
    incoming = lax.all_to_all(outgoing, "shard", split_axis=0, concat_axis=0, tiled=True)
    wanted = shard_index * blocks + jnp.arange(blocks, dtype=jnp.int32)
    receiver = (jnp.transpose(slot_table) == wanted[:, None]).astype(jnp.bfloat16)
    owned_rows = jnp.einsum(
        "ks,src->krc", receiver, incoming, preferred_element_type=jnp.float32
    ).astype(jnp.bfloat16)
    gathered = lax.all_gather(owned_rows, "rep", axis=1, tiled=True)
    left_new = (
        decay_rate * left_stat
        + jnp.einsum("krc,kjc->krj", owned_rows, gathered, preferred_element_type=jnp.float32)
        / block_order
    )
    column_share = lax.dynamic_slice_in_dim(gathered, rep_index * row_count, row_count, 2)
    right_new = (
        decay_rate * right_stat
        + jnp.einsum("kic,kij->kcj", column_share, gathered, preferred_element_type=jnp.float32)
        / block_order
    )
    fresh_slot = owner_slot[refresh[0]]
    holder = fresh_slot // blocks
    slot_index = fresh_slot % blocks
    owns_fresh = holder == shard_index
    fresh_pair = jnp.stack(
        [
            lax.dynamic_index_in_dim(left_new, slot_index, 0, keepdims=False),
            lax.dynamic_index_in_dim(right_new, slot_index, 0, keepdims=False),
        ]
    )
    fresh_whole = lax.all_gather(fresh_pair, "rep", axis=1, tiled=True)
    fresh_left, fresh_right = lax.cond(owns_fresh, both_roots, empty_roots, fresh_whole)
    fresh_rows = lax.dynamic_slice_in_dim(fresh_left, rep_index * row_count, row_count, 0)
    left_updated = lax.dynamic_update_index_in_dim(left_root, fresh_rows, slot_index, 0)
    left_root_new = jnp.where(owns_fresh, left_updated, left_root)
    right_updated = lax.dynamic_update_index_in_dim(right_root, fresh_right, slot_index, 0)
    right_root_new = jnp.where(owns_fresh, right_updated, right_root)
    half_step = jnp.einsum(
        "kri,kic->krc", left_root_new, gathered, preferred_element_type=jnp.float32
    ).astype(jnp.bfloat16)
    preconditioned = jnp.einsum(
        "kri,kic->krc", half_step, right_root_new, preferred_element_type=jnp.float32
    ).astype(jnp.bfloat16)
    direction = lax.all_gather(preconditioned, "rep", axis=1, tiled=True)
    return (left_new, right_new, left_root_new, right_root_new, direction)


MESH = pl.DeviceIdType.MESH


def exchange_kernel(
    reps,
    shards,
    slots_ref,
    refresh_ref,
    grads_ref,
    left_ref,
    left_stat_ref,
    right_stat_ref,
    owned_ref,
    grad_full,
    left_full,
    stat_full,
    stat_ref,
    quarter_in,
    quarter,
    pieces,
    share,
    outgoing,
    incoming,
    sum_send,
    sum_recv,
    swap_send,
    swap_recv,
    part_send,
    part_recv,
    spread_send,
    spread_recv,
    line_send,
    line_recv,
    local_sem,
):
    blocks = grads_ref.shape[1]
    rows = grads_ref.shape[2] // reps
    length = reps // 2
    me = lax.axis_index("rep")
    shard = lax.axis_index("shard")
    place = me // 2
    side = me % 2
    partner = place * 2 + (1 - side)

    def span(index):
        return pl.ds(pl.multiple_of(index * rows, rows), rows)

    slot = slots_ref[refresh_ref[0]] % blocks
    keeper = slots_ref[refresh_ref[0]] // blocks
    part = rows // shards
    for index in range(shards):
        part_rows = pl.ds(index * part, part)
        stat_ref[index, 0] = left_stat_ref[slot, part_rows, :].astype(jnp.bfloat16)
        stat_ref[index, 1] = right_stat_ref[slot, part_rows, :].astype(jnp.bfloat16)

    barrier = pltpu.get_barrier_semaphore()
    for step in range(1, reps):
        pl.semaphore_signal(
            barrier, inc=1, device_id=((me + step) % reps, shard), device_id_type=MESH
        )
    for step in range(1, shards):
        pl.semaphore_signal(
            barrier, inc=1, device_id=(me, (shard + step) % shards), device_id_type=MESH
        )
    pl.semaphore_wait(barrier, reps + shards - 2)

    def to_shards(source, target, send_sem, recv_sem):
        copies = []
        for step in range(1, shards):
            peer = (shard + step) % shards
            copies.append(
                pltpu.make_async_remote_copy(
                    src_ref=source(peer),
                    dst_ref=target,
                    send_sem=send_sem.at[step],
                    recv_sem=recv_sem.at[step],
                    device_id=(me, peer),
                    device_id_type=MESH,
                )
            )
        return copies

    sums = []

    def send_sums(steps):
        for step in steps:
            peer = (me + step) % reps
            copy = pltpu.make_async_remote_copy(
                src_ref=grads_ref.at[0, :, span(peer), :],
                dst_ref=pieces.at[me],
                send_sem=sum_send.at[step],
                recv_sem=sum_recv.at[step],
                device_id=(peer, shard),
                device_id_type=MESH,
            )
            copy.start()
            sums.append(copy)

    fulls = (left_full, stat_full, grad_full)

    def spots(array, source):
        if array == 1:
            return stat_full.at[:, source, shard]
        return fulls[array].at[:, span(source), :]

    def line_copy(array, source, way, target, first):
        where = spots(array, source)
        origin = first if first is not None else where
        return pltpu.make_async_remote_copy(
            src_ref=origin,
            dst_ref=where,
            send_sem=line_send.at[array, source, way],
            recv_sem=line_recv.at[array, source],
            device_id=(target, shard),
            device_id_type=MESH,
        )

    ways = ((0, 1), (1, -1))

    def send_line(array, source, way, delta, first):
        inside = (place + delta >= 0) & (place + delta < length)

        @pl.when(inside)
        def _():
            line_copy(array, source, way, me + 2 * delta, first).start()

    def wait_line(array, source, way, delta, first):
        inside = (place + delta >= 0) & (place + delta < length)

        @pl.when(inside)
        def _():
            line_copy(array, source, way, me + 2 * delta, first).wait_send()

    def begin(array, first):
        for way, delta in ways:
            send_line(array, me, way, delta, first)
        line_copy(array, me, 2, partner, first).start()

    def forward(array, hop):
        for way, delta in ways:
            origin = place - delta * hop

            @pl.when((origin >= 0) & (origin < length))
            def _():
                source = origin * 2 + side
                line_copy(array, source, 2, partner, None).wait_recv()
                send_line(array, source, way, delta, None)
                line_copy(array, source, 2, partner, None).start()

    def finish(array, first):
        if array != 1:
            for other in range(length):
                line_copy(array, other * 2 + 1 - side, 2, partner, None).wait_recv()
        for way, delta in ways:
            wait_line(array, me, way, delta, first)
        line_copy(array, me, 2, partner, first).wait_send()
        for hop in range(1, length):
            for way, delta in ways:
                origin = place - delta * hop

                @pl.when((origin >= 0) & (origin < length))
                def _():
                    source = origin * 2 + side
                    wait_line(array, source, way, delta, None)
                    line_copy(array, source, 2, partner, None).wait_send()

    parts = to_shards(lambda peer: stat_ref.at[peer], quarter_in.at[shard], part_send, part_recv)
    for copy in parts:
        copy.start()
    begin(0, left_ref)
    own_left = pltpu.make_async_copy(left_ref, spots(0, me), local_sem.at[0])
    own_left.start()
    send_sums(range(1, min(4, reps)))
    quarter_in[shard] = stat_ref[shard]
    for copy in parts:
        copy.wait_recv()
    quarter[...] = quarter_in[keeper]
    begin(1, quarter)
    own_stat = pltpu.make_async_copy(quarter, spots(1, me), local_sem.at[1])
    own_stat.start()
    send_sums(range(4, min(6, reps)))
    if length > 1:
        forward(1, 1)
        forward(0, 1)
    send_sums(range(6, reps))
    if length > 2:
        forward(1, 2)
        forward(0, 2)

    pieces[me] = grads_ref[0, :, span(me), :]
    for copy in sums:
        copy.wait_recv()
    for block in range(blocks):
        total = pieces[0, block].astype(jnp.float32)
        for index in range(1, reps):
            total = total + pieces[index, block].astype(jnp.float32)
        share[block] = total.astype(jnp.bfloat16)

    for target in range(shards):
        chosen = jnp.int32(0)
        for block in range(1, blocks):
            chosen = jnp.where(
                slots_ref[shard * blocks + block] // blocks == target, jnp.int32(block), chosen
            )
        outgoing[target] = share[chosen]
    swaps = to_shards(lambda peer: outgoing.at[peer], incoming.at[shard], swap_send, swap_recv)
    for copy in swaps:
        copy.start()
    incoming[shard] = outgoing[shard]
    for copy in swaps:
        copy.wait_recv()
    for block in range(blocks):
        holder = jnp.int32(0)
        for origin in range(1, shards):
            holder = jnp.where(
                slots_ref[origin * blocks + block] == shard * blocks + block,
                jnp.int32(origin),
                holder,
            )
        value = incoming[holder]
        owned_ref[block] = value
    begin(2, owned_ref)
    own_grad = pltpu.make_async_copy(owned_ref, spots(2, me), local_sem.at[2])
    own_grad.start()
    for hop in range(3, length):
        forward(1, hop)
        forward(0, hop)
    own_stat.wait()
    for other in range(length):
        line_copy(1, other * 2 + 1 - side, 2, partner, None).wait_recv()
    spreads = to_shards(
        lambda peer: stat_full.at[:, :, shard], stat_full.at[:, :, shard], spread_send, spread_recv
    )
    for copy in spreads:
        copy.start()
    for hop in range(1, length):
        forward(2, hop)
    for array, first in enumerate((left_ref, quarter, owned_ref)):
        finish(array, first)
    own_left.wait()
    own_grad.wait()
    for copy in spreads:
        copy.wait_recv()
    for copy in sums + swaps + parts + spreads:
        copy.wait_send()


def exchange(owner_slot, refresh, grads, left_root, left_stat, right_stat, reps, shards):
    blocks, order = grads.shape[1], grads.shape[2]
    rows = order // reps
    low = jnp.bfloat16
    vmem = pl.BlockSpec(memory_space=pltpu.VMEM)
    smem = pl.BlockSpec(memory_space=pltpu.SMEM)
    hbm = pl.BlockSpec(memory_space=pl.ANY)
    return pl.pallas_call(
        functools.partial(exchange_kernel, reps, shards),
        out_shape=(
            jax.ShapeDtypeStruct((blocks, rows, order), low),
            jax.ShapeDtypeStruct((blocks, order, order), low),
            jax.ShapeDtypeStruct((blocks, order, order), low),
            jax.ShapeDtypeStruct((2, reps, shards, rows // shards, order), low),
        ),
        in_specs=[smem, smem, vmem, vmem, vmem, vmem],
        out_specs=(vmem, hbm, hbm, hbm),
        scratch_shapes=[
            pltpu.VMEM((shards, 2, rows // shards, order), low),
            pltpu.VMEM((shards, 2, rows // shards, order), low),
            pltpu.VMEM((2, rows // shards, order), low),
            pltpu.VMEM((reps, blocks, rows, order), low),
            pltpu.VMEM((blocks, rows, order), low),
            pltpu.VMEM((shards, rows, order), low),
            pltpu.VMEM((shards, rows, order), low),
            pltpu.SemaphoreType.DMA((reps,)),
            pltpu.SemaphoreType.DMA((reps,)),
            pltpu.SemaphoreType.DMA((shards,)),
            pltpu.SemaphoreType.DMA((shards,)),
            pltpu.SemaphoreType.DMA((shards,)),
            pltpu.SemaphoreType.DMA((shards,)),
            pltpu.SemaphoreType.DMA((shards,)),
            pltpu.SemaphoreType.DMA((shards,)),
            pltpu.SemaphoreType.DMA((3, reps, 3)),
            pltpu.SemaphoreType.DMA((3, reps)),
            pltpu.SemaphoreType.DMA((3,)),
        ],
        compiler_params=pltpu.CompilerParams(collective_id=0, has_side_effects=True),
    )(owner_slot, refresh, grads, left_root, left_stat, right_stat)


def dot(left, right, dims=(1, 0)):
    return lax.dot_general(
        left, right, (((dims[0],), (dims[1],)), ((), ())), preferred_element_type=jnp.float32
    )


def precondition_kernel(
    slots_ref,
    refresh_ref,
    owned_ref,
    grad_full,
    left_full,
    stat_full,
    left_stat_ref,
    right_stat_ref,
    left_ref,
    right_ref,
    left_new_ref,
    right_new_ref,
    left_root_ref,
    right_root_ref,
    direction_ref,
    turned,
    fresh_left,
):
    blocks, rows, order = owned_ref.shape
    me = lax.axis_index("rep")
    shard = lax.axis_index("shard")
    mine = pl.ds(pl.multiple_of(me * rows, rows), rows)
    fresh_slot = slots_ref[refresh_ref[0]]
    slot = fresh_slot % blocks
    owns = fresh_slot // blocks == shard
    for block in range(blocks):
        grad = grad_full[block]
        turned[block] = grad.T
        left_new_ref[block] = (
            decay_rate * left_stat_ref[block] + dot(owned_ref[block], grad, (1, 1)) / order
        )
        right_new_ref[block] = (
            decay_rate * right_stat_ref[block] + dot(turned[block, mine, :], grad) / order
        )
    left_root_ref[...] = left_ref[...]
    right_root_ref[...] = right_ref[...]

    @pl.when(owns)
    def _():
        grad = grad_full[slot]
        grad_turned = turned[slot]
        left = decay_rate * stat_full[0].astype(jnp.float32) + dot(grad, grad_turned) / order
        right = decay_rate * stat_full[1].astype(jnp.float32) + dot(grad_turned, grad) / order
        fresh_left[...] = inverse_root(left)
        left_root_ref[slot] = fresh_left[mine, :]
        right_root_ref[slot] = inverse_root(right)

    for block in range(blocks):
        replaced = owns & (slot == block)

        @pl.when(replaced)
        def _():
            half = dot(fresh_left[...], grad_full[block]).astype(jnp.bfloat16)
            direction_ref[block] = half

        @pl.when(jnp.logical_not(replaced))
        def _():
            half = dot(left_full[block], grad_full[block]).astype(jnp.bfloat16)
            direction_ref[block] = half

        direction_ref[block] = dot(direction_ref[block], right_root_ref[block]).astype(
            jnp.bfloat16
        )


def precondition(*operands):
    owned, grad_full = operands[2], operands[3]
    left_stat, left_root, right_root = operands[6], operands[8], operands[9]
    order = owned.shape[2]
    low = jnp.bfloat16
    vmem = pl.BlockSpec(memory_space=pltpu.VMEM)
    smem = pl.BlockSpec(memory_space=pltpu.SMEM)
    return pl.pallas_call(
        precondition_kernel,
        out_shape=(
            jax.ShapeDtypeStruct(left_stat.shape, jnp.float32),
            jax.ShapeDtypeStruct(left_stat.shape, jnp.float32),
            jax.ShapeDtypeStruct(left_root.shape, low),
            jax.ShapeDtypeStruct(right_root.shape, low),
            jax.ShapeDtypeStruct(right_root.shape, low),
        ),
        in_specs=[smem, smem] + [vmem] * 8,
        out_specs=(vmem,) * 5,
        scratch_shapes=[pltpu.VMEM(grad_full.shape, low), pltpu.VMEM((order, order), low)],
    )(*operands)


def direct_body(grads, owner_slot, refresh, left_stat, right_stat, left_root, right_root):
    owned, grad_full, left_full, stat_full = exchange(
        owner_slot,
        refresh,
        grads,
        left_root,
        left_stat,
        right_stat,
        lax.axis_size("rep"),
        lax.axis_size("shard"),
    )
    order = grads.shape[2]
    stat_full = stat_full.reshape(2, order, order)
    gathered = (owned, grad_full, left_full, stat_full)
    return precondition(
        owner_slot, refresh, *gathered, left_stat, right_stat, left_root, right_root
    )


def choose(mesh, *arrays):
    reps = mesh.shape["rep"]
    rows = arrays[0].shape[2] // reps
    direct = reps % 2 == 0 and rows % (16 * mesh.shape["shard"]) == 0
    return (direct_body if direct else body)


def solution(mesh):
    def run(*arrays):
        return mapped(mesh, choose(mesh, *arrays))(*arrays)

    return run


def mapped(mesh, body):
    return jax.shard_map(
        body,
        mesh=mesh,
        in_specs=(
            P("rep", "shard", None, None),
            P(),
            P(),
            P("shard", "rep", None),
            P("shard", "rep", None),
            P("shard", "rep", None),
            P("shard", None, None),
        ),
        out_specs=(
            P("shard", "rep", None),
            P("shard", "rep", None),
            P("shard", "rep", None),
            P("shard", None, None),
            P("shard", None, None),
        ),
        check_vma=False,
    )
```

```python
import functools

import jax
import jax.numpy as jnp
from jax import lax
from jax.experimental import pallas as pl
from jax.experimental.pallas import tpu as pltpu
from jax.sharding import PartitionSpec as P

ITERS = 2


decay_rate = 0.95
epsilon_shift = 1e-06


def inverse_root(statistic):
    order = statistic.shape[0]
    identity = (
        lax.broadcasted_iota(jnp.int32, (order, order), 0)
        == lax.broadcasted_iota(jnp.int32, (order, order), 1)
    ).astype(jnp.float32)
    shifted = statistic + epsilon_shift * identity
    norm_scale = 2.5 / jnp.sqrt(jnp.sum(shifted * shifted))
    moment = norm_scale * shifted
    current = identity
    for number in range(ITERS):
        factor = (5.0 * identity - moment) * 0.25
        factor_low = factor.astype(jnp.bfloat16)
        if number == 0:
            current = jnp.sqrt(jnp.sqrt(norm_scale)) * factor
        else:
            current = jnp.dot(
                current.astype(jnp.bfloat16), factor_low, preferred_element_type=jnp.float32
            )
        if number + 1 < ITERS:
            square = jnp.dot(factor_low, factor_low, preferred_element_type=jnp.float32).astype(
                jnp.bfloat16
            )
            fourth = jnp.dot(square, square, preferred_element_type=jnp.float32).astype(
                jnp.bfloat16
            )
            moment = jnp.dot(
                fourth, moment.astype(jnp.bfloat16), preferred_element_type=jnp.float32
            )
    return current.astype(jnp.bfloat16)


def both_roots(fresh_whole):
    return (inverse_root(fresh_whole[0]), inverse_root(fresh_whole[1]))


def empty_roots(fresh_whole):
    blank = jnp.zeros(fresh_whole.shape[1:], jnp.bfloat16)
    return (blank, blank)


def body(grads, owner_slot, refresh, left_stat, right_stat, left_root, right_root):
    blocks = grads.shape[1]
    block_order = grads.shape[2]
    rep_count = lax.axis_size("rep")
    shards = lax.axis_size("shard")
    row_count = block_order // rep_count
    rep_index = lax.axis_index("rep")
    shard_index = lax.axis_index("shard")
    partial_value = grads[0].astype(jnp.float32)
    row_share = lax.psum_scatter(partial_value, "rep", scatter_dimension=1, tiled=True)
    row_share = row_share.astype(jnp.bfloat16)
    slot_table = owner_slot.reshape(shards, blocks)
    own_slots = lax.dynamic_index_in_dim(slot_table, shard_index, 0, keepdims=False)
    targets = own_slots // blocks
    selector = (targets[None, :] == jnp.arange(shards, dtype=jnp.int32)[:, None]).astype(
        jnp.bfloat16
    )
    outgoing = jnp.einsum(
        "ok,krc->orc", selector, row_share, preferred_element_type=jnp.float32
    ).astype(jnp.bfloat16)
    incoming = lax.all_to_all(outgoing, "shard", split_axis=0, concat_axis=0, tiled=True)
    wanted = shard_index * blocks + jnp.arange(blocks, dtype=jnp.int32)
    receiver = (jnp.transpose(slot_table) == wanted[:, None]).astype(jnp.bfloat16)
    owned_rows = jnp.einsum(
        "ks,src->krc", receiver, incoming, preferred_element_type=jnp.float32
    ).astype(jnp.bfloat16)
    gathered = lax.all_gather(owned_rows, "rep", axis=1, tiled=True)
    left_new = (
        decay_rate * left_stat
        + jnp.einsum("krc,kjc->krj", owned_rows, gathered, preferred_element_type=jnp.float32)
        / block_order
    )
    column_share = lax.dynamic_slice_in_dim(gathered, rep_index * row_count, row_count, 2)
    right_new = (
        decay_rate * right_stat
        + jnp.einsum("kic,kij->kcj", column_share, gathered, preferred_element_type=jnp.float32)
        / block_order
    )
    fresh_slot = owner_slot[refresh[0]]
    holder = fresh_slot // blocks
    slot_index = fresh_slot % blocks
    owns_fresh = holder == shard_index
    fresh_pair = jnp.stack(
        [
            lax.dynamic_index_in_dim(left_new, slot_index, 0, keepdims=False),
            lax.dynamic_index_in_dim(right_new, slot_index, 0, keepdims=False),
        ]
    )
    fresh_whole = lax.all_gather(fresh_pair, "rep", axis=1, tiled=True)
    fresh_left, fresh_right = lax.cond(owns_fresh, both_roots, empty_roots, fresh_whole)
    fresh_rows = lax.dynamic_slice_in_dim(fresh_left, rep_index * row_count, row_count, 0)
    left_updated = lax.dynamic_update_index_in_dim(left_root, fresh_rows, slot_index, 0)
    left_root_new = jnp.where(owns_fresh, left_updated, left_root)
    right_updated = lax.dynamic_update_index_in_dim(right_root, fresh_right, slot_index, 0)
    right_root_new = jnp.where(owns_fresh, right_updated, right_root)
    half_step = jnp.einsum(
        "kri,kic->krc", left_root_new, gathered, preferred_element_type=jnp.float32
    ).astype(jnp.bfloat16)
    preconditioned = jnp.einsum(
        "kri,kic->krc", half_step, right_root_new, preferred_element_type=jnp.float32
    ).astype(jnp.bfloat16)
    direction = lax.all_gather(preconditioned, "rep", axis=1, tiled=True)
    return (left_new, right_new, left_root_new, right_root_new, direction)


MESH = pl.DeviceIdType.MESH


def exchange_kernel(
    reps,
    shards,
    slots_ref,
    refresh_ref,
    grads_ref,
    left_ref,
    left_stat_ref,
    right_stat_ref,
    grad_full,
    left_full,
    left_new_ref,
    right_new_ref,
    fresh_left_ref,
    fresh_right_ref,
    owned_ref,
    stat_full,
    turned,
    stat_ref,
    quarter_in,
    quarter,
    pieces,
    share,
    incoming,
    sum_send,
    sum_recv,
    swap_send,
    swap_recv,
    part_send,
    part_recv,
    spread_send,
    spread_recv,
    line_send,
    line_recv,
    local_sem,
):
    blocks = grads_ref.shape[1]
    order = grads_ref.shape[2]
    rows = order // reps
    length = reps // 2
    me = lax.axis_index("rep")
    shard = lax.axis_index("shard")
    place = me // 2
    side = me % 2
    partner = place * 2 + (1 - side)

    def span(index):
        return pl.ds(pl.multiple_of(index * rows, rows), rows)

    slot = slots_ref[refresh_ref[0]] % blocks
    keeper = slots_ref[refresh_ref[0]] // blocks
    part = rows // shards
    for index in range(shards):
        part_rows = pl.ds(index * part, part)
        stat_ref[index, 0] = left_stat_ref[slot, part_rows, :].astype(jnp.bfloat16)
        stat_ref[index, 1] = right_stat_ref[slot, part_rows, :].astype(jnp.bfloat16)

    barrier = pltpu.get_barrier_semaphore()
    for step in range(1, reps):
        pl.semaphore_signal(
            barrier, inc=1, device_id=((me + step) % reps, shard), device_id_type=MESH
        )
    for step in range(1, shards):
        pl.semaphore_signal(
            barrier, inc=1, device_id=(me, (shard + step) % shards), device_id_type=MESH
        )
    pl.semaphore_wait(barrier, reps + shards - 2)

    def to_shards(source, target, send_sem, recv_sem):
        copies = []
        for step in range(1, shards):
            peer = (shard + step) % shards
            copies.append(
                pltpu.make_async_remote_copy(
                    src_ref=source(peer),
                    dst_ref=target,
                    send_sem=send_sem.at[step],
                    recv_sem=recv_sem.at[step],
                    device_id=(me, peer),
                    device_id_type=MESH,
                )
            )
        return copies

    sums = [[] for block in range(blocks)]

    def send_sums(block):
        for step in range(1, reps):
            peer = (me + step) % reps
            copy = pltpu.make_async_remote_copy(
                src_ref=grads_ref.at[0, block, span(peer), :],
                dst_ref=pieces.at[me, block],
                send_sem=sum_send.at[block, step],
                recv_sem=sum_recv.at[block, step],
                device_id=(peer, shard),
                device_id_type=MESH,
            )
            copy.start()
            sums[block].append(copy)

    def spots(array, source):
        if array == 1:
            return stat_full.at[:, source, shard]
        if array == 0:
            return left_full.at[:, span(source), :]
        return grad_full.at[array - 2, span(source), :]

    def line_copy(array, source, way, target, first):
        where = spots(array, source)
        origin = first if first is not None else where
        return pltpu.make_async_remote_copy(
            src_ref=origin,
            dst_ref=where,
            send_sem=line_send.at[array, source, way],
            recv_sem=line_recv.at[array, source],
            device_id=(target, shard),
            device_id_type=MESH,
        )

    ways = ((0, 1), (1, -1))

    def send_line(array, source, way, delta, first):
        inside = (place + delta >= 0) & (place + delta < length)

        @pl.when(inside)
        def _():
            line_copy(array, source, way, me + 2 * delta, first).start()

    def wait_line(array, source, way, delta, first):
        inside = (place + delta >= 0) & (place + delta < length)

        @pl.when(inside)
        def _():
            line_copy(array, source, way, me + 2 * delta, first).wait_send()

    def begin(array, first):
        for way, delta in ways:
            send_line(array, me, way, delta, first)
        line_copy(array, me, 2, partner, first).start()

    def forward(array, hop):
        for way, delta in ways:
            origin = place - delta * hop

            @pl.when((origin >= 0) & (origin < length))
            def _():
                source = origin * 2 + side
                line_copy(array, source, 2, partner, None).wait_recv()
                send_line(array, source, way, delta, None)
                line_copy(array, source, 2, partner, None).start()

    def finish(array, first):
        if array == 0:
            for other in range(length):
                line_copy(array, other * 2 + 1 - side, 2, partner, None).wait_recv()
        for way, delta in ways:
            wait_line(array, me, way, delta, first)
        line_copy(array, me, 2, partner, first).wait_send()
        for hop in range(1, length):
            for way, delta in ways:
                origin = place - delta * hop

                @pl.when((origin >= 0) & (origin < length))
                def _():
                    source = origin * 2 + side
                    wait_line(array, source, way, delta, None)
                    line_copy(array, source, 2, partner, None).wait_send()

    parts = to_shards(lambda peer: stat_ref.at[peer], quarter_in.at[shard], part_send, part_recv)
    for copy in parts:
        copy.start()
    for block in range(blocks):
        send_sums(block)
    begin(0, left_ref)
    own_left = pltpu.make_async_copy(left_ref, spots(0, me), local_sem.at[0])
    own_left.start()
    quarter_in[shard] = stat_ref[shard]
    for copy in parts:
        copy.wait_recv()
    quarter[...] = quarter_in[keeper]
    begin(1, quarter)
    own_stat = pltpu.make_async_copy(quarter, spots(1, me), local_sem.at[1])
    own_stat.start()
    pieces[me] = grads_ref[0, :, span(me), :]
    swaps = []

    def add_up(block):
        for copy in sums[block]:
            copy.wait_recv()
        total = pieces[0, block].astype(jnp.float32)
        for index in range(1, reps):
            total = total + pieces[index, block].astype(jnp.float32)
        share[block] = total.astype(jnp.bfloat16)
        copies = to_shards(
            lambda peer: share.at[block],
            incoming.at[block, shard],
            swap_send.at[block],
            swap_recv.at[block],
        )
        for copy in copies:
            copy.start()
        swaps.append(copies)
        incoming[block, shard] = share[block]

    def take(block):
        for copy in swaps[block]:
            copy.wait_recv()
        value = incoming[block, 0]
        for origin in range(1, shards):
            held = slots_ref[origin * blocks + block] == shard * blocks + block
            value = jnp.where(held, incoming[block, origin], value)
        owned_ref[block] = value
        begin(2 + block, owned_ref.at[block])

    for block in range(blocks):
        add_up(block)
        if block > 0:
            take(block - 1)
    take(blocks - 1)
    own_grad = pltpu.make_async_copy(owned_ref, grad_full.at[:, span(me), :], local_sem.at[2])
    own_grad.start()
    for hop in range(1, length):
        forward(1, hop)
        for array in range(2, 2 + blocks):
            forward(array, hop)
    own_stat.wait()
    for other in range(length):
        line_copy(1, other * 2 + 1 - side, 2, partner, None).wait_recv()
    spreads = to_shards(
        lambda peer: stat_full.at[:, :, shard], stat_full.at[:, :, shard], spread_send, spread_recv
    )
    for copy in spreads:
        copy.start()
    own_grad.wait()
    if length > 1:
        forward(0, 1)
    for block in range(blocks):
        for other in range(length):
            line_copy(2 + block, other * 2 + 1 - side, 2, partner, None).wait_recv()
    if length > 2:
        forward(0, 2)
    for block in range(blocks):
        grad = grad_full[block]
        turned[block] = grad.T
        left_new_ref[block] = (
            decay_rate * left_stat_ref[block] + dot(owned_ref[block], grad, (1, 1)) / order
        )
        right_new_ref[block] = (
            decay_rate * right_stat_ref[block] + dot(turned[block, span(me), :], grad) / order
        )
    for hop in range(3, length):
        forward(0, hop)
    for copy in spreads:
        copy.wait_recv()
    grad = grad_full[slot]
    grad_turned = turned[slot]
    left_sum = stat_full[0].reshape(order, order).astype(jnp.float32)
    right_sum = stat_full[1].reshape(order, order).astype(jnp.float32)
    fresh_left_ref[...] = inverse_root(decay_rate * left_sum + dot(grad, grad_turned) / order)
    fresh_right_ref[...] = inverse_root(decay_rate * right_sum + dot(grad_turned, grad) / order)
    finish(0, left_ref)
    finish(1, quarter)
    for block in range(blocks):
        finish(2 + block, owned_ref.at[block])
    own_left.wait()
    for copies in sums + swaps + [parts, spreads]:
        for copy in copies:
            copy.wait_send()


def exchange(owner_slot, refresh, grads, left_root, left_stat, right_stat, reps, shards):
    blocks, order = grads.shape[1], grads.shape[2]
    rows = order // reps
    low = jnp.bfloat16
    vmem = pl.BlockSpec(memory_space=pltpu.VMEM)
    smem = pl.BlockSpec(memory_space=pltpu.SMEM)
    hbm = pl.BlockSpec(memory_space=pl.ANY)
    return pl.pallas_call(
        functools.partial(exchange_kernel, reps, shards),
        out_shape=(
            jax.ShapeDtypeStruct((blocks, order, order), low),
            jax.ShapeDtypeStruct((blocks, order, order), low),
            jax.ShapeDtypeStruct((blocks, rows, order), jnp.float32),
            jax.ShapeDtypeStruct((blocks, rows, order), jnp.float32),
            jax.ShapeDtypeStruct((order, order), low),
            jax.ShapeDtypeStruct((order, order), low),
        ),
        in_specs=[smem, smem, vmem, vmem, vmem, vmem],
        out_specs=(vmem, hbm, vmem, vmem, vmem, vmem),
        scratch_shapes=[
            pltpu.VMEM((blocks, rows, order), low),
            pltpu.VMEM((2, reps, shards, rows // shards, order), low),
            pltpu.VMEM((blocks, order, order), low),
            pltpu.VMEM((shards, 2, rows // shards, order), low),
            pltpu.VMEM((shards, 2, rows // shards, order), low),
            pltpu.VMEM((2, rows // shards, order), low),
            pltpu.VMEM((reps, blocks, rows, order), low),
            pltpu.VMEM((blocks, rows, order), low),
            pltpu.VMEM((blocks, shards, rows, order), low),
            pltpu.SemaphoreType.DMA((blocks, reps)),
            pltpu.SemaphoreType.DMA((blocks, reps)),
            pltpu.SemaphoreType.DMA((blocks, shards)),
            pltpu.SemaphoreType.DMA((blocks, shards)),
            pltpu.SemaphoreType.DMA((shards,)),
            pltpu.SemaphoreType.DMA((shards,)),
            pltpu.SemaphoreType.DMA((shards,)),
            pltpu.SemaphoreType.DMA((shards,)),
            pltpu.SemaphoreType.DMA((2 + blocks, reps, 3)),
            pltpu.SemaphoreType.DMA((2 + blocks, reps)),
            pltpu.SemaphoreType.DMA((3,)),
        ],
        compiler_params=pltpu.CompilerParams(collective_id=0, has_side_effects=True),
    )(owner_slot, refresh, grads, left_root, left_stat, right_stat)


def dot(left, right, dims=(1, 0)):
    return lax.dot_general(
        left, right, (((dims[0],), (dims[1],)), ((), ())), preferred_element_type=jnp.float32
    )


def precondition_kernel(
    slots_ref,
    refresh_ref,
    grad_full,
    left_full,
    new_left_ref,
    new_right_ref,
    left_ref,
    right_ref,
    left_root_ref,
    right_root_ref,
    direction_ref,
):
    blocks, rows, order = left_ref.shape
    me = lax.axis_index("rep")
    shard = lax.axis_index("shard")
    mine = pl.ds(pl.multiple_of(me * rows, rows), rows)
    fresh_slot = slots_ref[refresh_ref[0]]
    slot = fresh_slot % blocks
    owns = fresh_slot // blocks == shard
    left_root_ref[...] = left_ref[...]
    right_root_ref[...] = right_ref[...]

    @pl.when(owns)
    def _():
        left_root_ref[slot] = new_left_ref[mine, :]
        right_root_ref[slot] = new_right_ref[...]

    for block in range(blocks):
        replaced = owns & (slot == block)

        @pl.when(replaced)
        def _():
            direction_ref[block] = dot(new_left_ref[...], grad_full[block]).astype(jnp.bfloat16)

        @pl.when(jnp.logical_not(replaced))
        def _():
            direction_ref[block] = dot(left_full[block], grad_full[block]).astype(jnp.bfloat16)

        direction_ref[block] = dot(direction_ref[block], right_root_ref[block]).astype(
            jnp.bfloat16
        )


def precondition(*operands):
    left_root, right_root = operands[6], operands[7]
    low = jnp.bfloat16
    vmem = pl.BlockSpec(memory_space=pltpu.VMEM)
    smem = pl.BlockSpec(memory_space=pltpu.SMEM)
    return pl.pallas_call(
        precondition_kernel,
        out_shape=(
            jax.ShapeDtypeStruct(left_root.shape, low),
            jax.ShapeDtypeStruct(right_root.shape, low),
            jax.ShapeDtypeStruct(right_root.shape, low),
        ),
        in_specs=[smem, smem] + [vmem] * 6,
        out_specs=(vmem,) * 3,
    )(*operands)


def direct_body(grads, owner_slot, refresh, left_stat, right_stat, left_root, right_root):
    grad_full, left_full, left_new, right_new, fresh_left, fresh_right = exchange(
        owner_slot,
        refresh,
        grads,
        left_root,
        left_stat,
        right_stat,
        lax.axis_size("rep"),
        lax.axis_size("shard"),
    )
    roots = precondition(
        owner_slot, refresh, grad_full, left_full, fresh_left, fresh_right, left_root, right_root
    )
    return (left_new, right_new, *roots)


def choose(mesh, *arrays):
    reps = mesh.shape["rep"]
    rows = arrays[0].shape[2] // reps
    direct = reps % 2 == 0 and rows % (16 * mesh.shape["shard"]) == 0
    return (direct_body if direct else body)


def solution(mesh):
    def run(*arrays):
        return mapped(mesh, choose(mesh, *arrays))(*arrays)

    return run


def mapped(mesh, body):
    return jax.shard_map(
        body,
        mesh=mesh,
        in_specs=(
            P("rep", "shard", None, None),
            P(),
            P(),
            P("shard", "rep", None),
            P("shard", "rep", None),
            P("shard", "rep", None),
            P("shard", None, None),
        ),
        out_specs=(
            P("shard", "rep", None),
            P("shard", "rep", None),
            P("shard", "rep", None),
            P("shard", None, None),
            P("shard", None, None),
        ),
        check_vma=False,
    )
```
